512 devices in a mesh: leaf: 32 (over y, x), grp: 16 (over z, core).
Axes of the slice: x: 4, y: 8, z: 8, core: 2. Of those that a mesh axis runs over, the one named last changes fastest.
Arguments:
- low_rhs: float32 [32768, 4096], P('leaf', 'grp'), may hold values from -6 to 6
- low_inverse: float32 [32768, 1024], P(('leaf', 'grp')), as said below
- panels: float32 [32768, 1024], P(('leaf', 'grp')), may hold values from -0.1875 to 0.1875
- row_blocks: int32 [32, 8], P('leaf'), may hold values from 0 to 15, all different within a row
- root_rhs: float32 [2048, 4096], P('leaf', 'grp'), may hold values from -6 to 6
- root_inverse: float32 [2048, 2048], P('leaf'), as said below
Outputs:
- low_solution: float32 [32768, 4096], P('leaf', 'grp')
- root_solution: float32 [2048, 4096], P('leaf', 'grp')
The draws below stay inside these ranges and needn't reach their ends.
Inputs may be any that keep to these rules, and one draw needn't show every extreme that they name: `row_blocks`: each row names 8 different root blocks, and every root block is named by some row. `low_inverse`: lower triangular, with a positive diagonal. `root_inverse`: lower triangular, with a positive diagonal.
All inputs are finite; a program needn't handle non-finite values.
Results may differ from the reference program's by a relative error of at most 0.0003.
Values sent between devices are 32-bit elements; how exact they have to be, the bound alone decides.
No kernel may reach another device: no remote copies, remote signals or barrier semaphores. Data moves between devices by JAX's collectives and lax.ppermute only.
A program may use at most 64 MiB of HBM per device.

```python
import jax
import jax.numpy as jnp
from jax import lax

W = 1024
BLK = 128
NB = 16
K = 8
NS = 32
WR = 2048
SAMPLES = 4096


def triangle(key, count, width):
    key_diag, key_off = jax.random.split(key)
    rows = jnp.arange(width)[:, None]
    cols = jnp.arange(width)[None, :]
    diag_vals = jnp.exp(jax.random.uniform(key_diag, (count, width, 1), jnp.float32, jnp.log(0.5), jnp.log(2.0)))
    off_vals = jax.random.normal(key_off, (count, width, width), jnp.float32)
    off_vals = off_vals * (0.6 / jnp.sqrt(width * 1.0))
    lower = jnp.where(cols < rows, off_vals, 0.0)
    return lower + jnp.where(cols == rows, diag_vals, 0.0)


def draw_low_inverse(key, part):
    return triangle(jax.random.fold_in(key, 11), NS, W).reshape(NS * W, W)


def draw_root_inverse(key, part):
    return triangle(jax.random.fold_in(key, 23), 1, WR).reshape(WR, WR)


def levels(own_key, dims, cuts, least, top_value):
    gain, own = 1.0, jax.random.fold_in(own_key, 6)
    for dim, shards_of in cuts:
        draws = jnp.exp(jax.random.uniform(jax.random.fold_in(own, dim), (shards_of,), jnp.float32, least / len(cuts), top_value / len(cuts)))
        gain = gain * jnp.repeat(draws, dims[dim] // shards_of).reshape([-1 if axis == dim else 1 for axis in range(len(dims))])
    return gain


def distinct(own_key, rows, number_of, top, lift):
    ranking = jax.random.permutation(jax.random.fold_in(own_key, 1), number_of)
    boost = ranking
    for power in range(3):
        boost = boost * boost // number_of
    boost = boost * lift // number_of
    lots = jax.random.randint(jax.random.fold_in(own_key, 2), (rows, number_of), 0, 4096) + boost
    sure = jax.random.permutation(jax.random.fold_in(own_key, 3), rows)[jnp.arange(number_of) % rows]
    lots = jnp.where(jnp.arange(rows)[:, None] == sure[None, :], 1 << 14, lots)
    score = lots * number_of + jnp.arange(number_of)
    return lax.top_k(score.astype(jnp.int32), top)[1].astype(jnp.int32)


def normal_values(stream_key, extent, deviation, most, cuts=(), dtype=jnp.bfloat16):
    drawn = deviation * jax.random.normal(stream_key, extent, jnp.float32)
    if cuts:
        drawn = drawn * levels(stream_key, extent, cuts, -0.22, 0.18)
    return jnp.clip(drawn, -most, most).astype(dtype)


def setup_inputs(seed: int = 0) -> dict:
    key_of = jax.random.split(jax.random.key(seed), 7)
    low_rhs = normal_values(key_of[0], (NS * W, SAMPLES), 1.0, 6.0, ((0, 32), (1, 16)), jnp.float32)
    low_inverse = draw_low_inverse(jax.random.fold_in(key_of[6], 71), 0)
    panels = normal_values(key_of[2], (NS * K * BLK, W), W ** -0.5, 0.1875, ((0, 512),), jnp.float32)
    row_blocks = distinct(key_of[3], NS, NB, K, 0)
    root_rhs = normal_values(key_of[4], (WR, SAMPLES), 1.0, 6.0, ((0, 32), (1, 16)), jnp.float32)
    root_inverse = draw_root_inverse(jax.random.fold_in(key_of[6], 71), 0)
    return dict(low_rhs=low_rhs, low_inverse=low_inverse, panels=panels, row_blocks=row_blocks, root_rhs=root_rhs, root_inverse=root_inverse)


def reference(low_rhs, low_inverse, panels, row_blocks, root_rhs, root_inverse):
    inverses = low_inverse.reshape(NS, W, W)
    rights = low_rhs.reshape(NS, W, SAMPLES)
    panel_set = panels.reshape(NS, K * BLK, W)

    def one_node(total, items):
        inverse_s, right_s, panel_s, blocks_s = items
        solved = jnp.dot(inverse_s, right_s, precision=lax.Precision.HIGHEST)
        update = jnp.dot(panel_s, solved, precision=lax.Precision.HIGHEST).reshape(K, BLK, SAMPLES)
        total = total.at[blocks_s.astype(jnp.int32)].add(update)
        return total, solved

    start = jnp.zeros((NB, BLK, SAMPLES), jnp.float32)
    total, solved_all = lax.scan(one_node, start, (inverses, rights, panel_set, row_blocks))
    combined = root_rhs - total.reshape(WR, SAMPLES)
    root_solution = jnp.dot(root_inverse, combined, precision=lax.Precision.HIGHEST)
    return solved_all.reshape(NS * W, SAMPLES), root_solution
```

```python
import jax
import jax.numpy as jnp
from jax import lax
from jax.sharding import Mesh
from jax.sharding import PartitionSpec as P

BLK = 128
NB = 16
K = 8
NY, NX, NZ, NC = 8, 4, 8, 2
LEAF = ("y", "x")
GRP = ("z", "c")


def mm(a, b):
    return jnp.dot(a, b, precision=lax.Precision.HIGH, preferred_element_type=jnp.float32)


def body(low_rhs, low_inverse, panels, row_blocks, root_rhs, root_inverse):
    width = low_rhs.shape[0]
    cols = low_rhs.shape[1]
    rows = low_inverse.shape[0]
    own = root_rhs.shape[0]

    by_x = root_inverse.reshape(own, NY, NX, own).transpose(2, 0, 1, 3).reshape(NX, own, NY * own)
    root_part = lax.all_to_all(by_x, "x", 0, 0).reshape(NX * own, NY * own)

    both = lax.all_gather(jnp.concatenate([low_inverse, panels]), GRP, axis=0)
    both, root_part = lax.optimization_barrier((both, root_part))
    low_solution = mm(both[:, :rows].reshape(width, width), low_rhs)
    update = mm(both[:, rows:].reshape(width, width), low_solution)

    onehot = (row_blocks[0][None, :] == jnp.arange(NB, dtype=jnp.int32)[:, None]).astype(jnp.float32)
    placed = jnp.dot(onehot, update.reshape(K, BLK * cols), precision=lax.Precision.HIGHEST)
    parts = lax.all_to_all(placed.reshape(NY * NX, own, cols), LEAF, 0, 0)
    combined = root_rhs - jnp.sum(parts, axis=0)

    column = lax.all_to_all(jnp.broadcast_to(combined[None], (NY, own, cols)), "y", 0, 0)
    partial = mm(root_part, column.reshape(NY * own, cols))
    pieces = lax.all_to_all(partial.reshape(NX, own, cols), "x", 0, 0)
    return (low_solution, jnp.sum(pieces, axis=0))


def solution(mesh):
    fine = Mesh(mesh.devices.reshape(NY, NX, NZ, NC), LEAF + GRP)
    placed = (
        P(LEAF, GRP),
        P(LEAF + GRP, None),
        P(LEAF + GRP, None),
        P(LEAF, None),
        P(LEAF, GRP),
        P(LEAF, None),
    )
    return jax.shard_map(
        body,
        mesh=fine,
        in_specs=placed,
        out_specs=(P(LEAF, GRP), P(LEAF, GRP)),
        check_vma=False,
    )
```

```python
import jax
import jax.numpy as jnp
from jax import lax
from jax.experimental import pallas as pl
from jax.experimental.pallas import tpu as pltpu
from jax.sharding import Mesh
from jax.sharding import PartitionSpec as P

BLK = 128
NB = 16
K = 8
NY, NX, NZ, NC = 8, 4, 8, 2
LEAF = ("y", "x")
GRP = ("z", "c")
SUB, LANE = 8, 128
VMEM = pl.BlockSpec(memory_space=pltpu.VMEM)
SMEM = pl.BlockSpec(memory_space=pltpu.SMEM)


def split(a):
    hi = a.astype(jnp.bfloat16)
    return hi, (a - hi.astype(jnp.float32)).astype(jnp.bfloat16)


def dot3(a, b_hi, b_lo):
    hi, lo = split(a)
    d = lambda u, v: jnp.dot(u, v, preferred_element_type=jnp.float32)
    return d(hi, b_hi) + (d(hi, b_lo) + d(lo, b_hi))


def solve_kernel(both_ref, rhs_ref, low_ref, tiles_ref, r_hi, r_lo, s_hi, s_lo):
    step = pl.program_id(0)
    rows = both_ref.shape[0] * both_ref.shape[1]

    @pl.when(step == 0)
    def _():
        r_hi[...], r_lo[...] = split(rhs_ref[...])

    for i in range(4):

        @pl.when(step == i)
        def _():
            deep = (i + 1) * rows
            a = both_ref[...].reshape(rows, both_ref.shape[2])[:, :deep]
            s = dot3(a, r_hi[:deep], r_lo[:deep])
            here = pl.ds(i * rows, rows)
            low_ref[here, :] = s
            s_hi[here, :], s_lo[here, :] = split(s)

    for i in range(4):

        @pl.when(step == 4 + i)
        def _():
            u = dot3(both_ref[...].reshape(rows, both_ref.shape[2]), s_hi[...], s_lo[...])
            for half in range(2):
                k = 2 * i + half
                for y in range(NY):
                    for x in range(NX):
                        r = BLK * half + SUB * (NY * (x % 2) + y)
                        c = LANE * (x // 2)
                        tiles_ref[NX * y + x, SUB * k : SUB * (k + 1), :] = u[r : r + SUB, c : c + LANE]


def solve(both, rhs):
    shards, rows2, width = both.shape
    rows, cols = rows2 // 2, rhs.shape[1]
    return pl.pallas_call(
        solve_kernel,
        grid=(8,),
        in_specs=[
            pl.BlockSpec((shards // 4, rows, width), lambda i: (i % 4, i // 4, 0)),
            pl.BlockSpec((width, cols), lambda i: (0, 0)),
        ],
        out_specs=[
            pl.BlockSpec((width, cols), lambda i: (0, 0)),
            pl.BlockSpec((NY * NX, K * SUB, LANE), lambda i: (0, 0, 0)),
        ],
        out_shape=[
            jax.ShapeDtypeStruct((width, cols), jnp.float32),
            jax.ShapeDtypeStruct((NY * NX, K * SUB, LANE), jnp.float32),
        ],
        scratch_shapes=[pltpu.VMEM((width, cols), jnp.bfloat16)] * 4,
        name="solve",
    )(both, rhs)


def collect_kernel(index_ref, start_ref, parts_ref, out_ref, acc):
    acc[...] = start_ref[...]

    def one(s, carry):
        at = [pl.multiple_of(index_ref[s, k] * SUB, SUB) for k in range(K)]
        new = [acc[pl.ds(at[k], SUB), :] - parts_ref[s, SUB * k : SUB * (k + 1), :] for k in range(K)]
        for k in range(K):
            acc[pl.ds(at[k], SUB), :] = new[k]
        return carry

    lax.fori_loop(0, parts_ref.shape[0], one, 0)
    for y in range(NY):
        out_ref[y] = acc[...]


def collect(index, start, parts):
    return pl.pallas_call(
        collect_kernel,
        in_specs=[SMEM, VMEM, VMEM],
        out_specs=VMEM,
        out_shape=jax.ShapeDtypeStruct((NY, NB * SUB, LANE), jnp.float32),
        scratch_shapes=[pltpu.VMEM((NB * SUB, LANE), jnp.float32)],
        name="collect",
    )(index, start, parts)


def root_kernel(inv_ref, column_ref, out_ref):
    tiles = [column_ref[y, SUB * b : SUB * (b + 1), :] for b in range(NB) for y in range(NY)]
    hi, lo = split(jnp.concatenate(tiles))
    out = dot3(inv_ref[...].reshape(-1, inv_ref.shape[2]), hi, lo)
    out_ref[...] = out.reshape(out_ref.shape)


def root(inv, column):
    return pl.pallas_call(
        root_kernel,
        in_specs=[VMEM, VMEM],
        out_specs=VMEM,
        out_shape=jax.ShapeDtypeStruct((inv.shape[0], inv.shape[1], LANE), jnp.float32),
        name="root",
    )(inv, column)


def body(low_rhs, low_inverse, panels, row_blocks, root_rhs, root_inverse):
    own = root_rhs.shape[0]
    parity = lax.axis_index("x") % 2

    by_parity = root_inverse.reshape(own, NB, 2, BLK // 2).transpose(2, 0, 1, 3).reshape(2, own, NB * BLK // 2)
    inv = lax.all_to_all(jnp.concatenate([by_parity, by_parity]), "x", 0, 0)
    rhs_tiles = root_rhs.reshape(NY, 1, SUB, 2, 1, LANE).transpose(0, 3, 4, 1, 2, 5)
    rhs_tiles = jnp.broadcast_to(rhs_tiles.reshape(NY, 2, 1, SUB, LANE), (NY, 2, 2, SUB, LANE))
    blocks = jnp.pad(row_blocks.astype(jnp.float32), ((0, SUB - 1), (0, LANE - K)))
    early = jnp.concatenate(
        [rhs_tiles.reshape(NY * NX, SUB, LANE), jnp.broadcast_to(blocks[None], (NY * NX, SUB, LANE))], axis=1
    )
    early = lax.all_to_all(early, LEAF, 0, 0)
    index = early[:, SUB, :K].astype(jnp.int32)
    start = lax.dynamic_index_in_dim(early[:, :SUB].reshape(NB, 2, SUB, LANE), parity, 1, keepdims=False)
    start = start.reshape(NB * SUB, LANE)

    both = lax.all_gather(jnp.concatenate([low_inverse, panels]), GRP, axis=0)
    both, inv, index, start = lax.optimization_barrier((both, inv, index, start))

    low_solution, tiles = solve(both, low_rhs)
    parts = lax.all_to_all(tiles, LEAF, 0, 0)
    column = lax.all_to_all(collect(index, start, parts), "y", 0, 0)
    pieces = lax.all_to_all(root(inv, column), "x", 0, 0)
    return (low_solution, jnp.concatenate([pieces[0] + pieces[1], pieces[2] + pieces[3]], axis=1))


def solution(mesh):
    fine = Mesh(mesh.devices.reshape(NY, NX, NZ, NC), LEAF + GRP)
    placed = (
        P(LEAF, GRP),
        P(LEAF + GRP, None),
        P(LEAF + GRP, None),
        P(LEAF, None),
        P(LEAF, GRP),
        P(LEAF, None),
    )
    return jax.shard_map(
        body,
        mesh=fine,
        in_specs=placed,
        out_specs=(P(LEAF, GRP), P(LEAF, GRP)),
        check_vma=False,
    )
```

```python
import jax
import jax.numpy as jnp
from jax import lax
from jax.experimental import pallas as pl
from jax.experimental.pallas import tpu as pltpu
from jax.sharding import Mesh
from jax.sharding import PartitionSpec as P

BLK = 128
NB = 16
K = 8
NY, NX, NZ, NC = 8, 4, 8, 2
LEAF = ("y", "x")
GRP = ("z", "c")
SUB, LANE = 8, 128
VMEM = pl.BlockSpec(memory_space=pltpu.VMEM)
SMEM = pl.BlockSpec(memory_space=pltpu.SMEM)


def split(a):
    hi = a.astype(jnp.bfloat16)
    return hi, (a - hi.astype(jnp.float32)).astype(jnp.bfloat16)


def dot3(a, b_hi, b_lo):
    hi, lo = split(a)
    d = lambda u, v: jnp.dot(u, v, preferred_element_type=jnp.float32)
    return d(hi, b_hi) + (d(hi, b_lo) + d(lo, b_hi))


def solve_kernel(both_ref, rhs_ref, low_ref, tiles_ref, l_buf, p_buf, s_hi, s_lo, sems):
    parts, shards, rows, width = l_buf.shape
    part = shards * rows

    def read(i):
        here = pl.ds(shards * (i % parts), shards)
        if i < parts:
            deep = pl.ds(0, (i + 1) * part)
            src, dst = both_ref.at[here, pl.ds(0, rows), deep], l_buf.at[i, :, :, deep]
        else:
            src, dst = both_ref.at[here, pl.ds(rows, rows), :], p_buf.at[i - parts]
        return pltpu.make_async_copy(src, dst, sems.at[i])

    reads = [read(i) for i in range(2 * parts)]
    for copy in reads:
        copy.start()
    r_hi, r_lo = split(rhs_ref[...])
    for i in range(parts):
        reads[i].wait()
        deep = (i + 1) * part
        s = dot3(l_buf[i].reshape(part, width)[:, :deep], r_hi[:deep], r_lo[:deep])
        here = pl.ds(i * part, part)
        low_ref[here, :] = s
        s_hi[here, :], s_lo[here, :] = split(s)
    for i in range(parts):
        reads[parts + i].wait()
        u = dot3(p_buf[i].reshape(part, width), s_hi[...], s_lo[...])
        for j in range(part // BLK):
            k = i * (part // BLK) + j
            for y in range(NY):
                for x in range(NX):
                    r = BLK * j + SUB * (NX * (y // 2) + x)
                    c = LANE * (y % 2)
                    tiles_ref[NX * y + x, SUB * k : SUB * (k + 1), :] = u[r : r + SUB, c : c + LANE]


def solve(both, rhs, parts=2):
    shards, rows2, width = both.shape
    rows, cols = rows2 // 2, rhs.shape[1]
    return pl.pallas_call(
        solve_kernel,
        in_specs=[pl.BlockSpec(memory_space=pltpu.HBM), VMEM],
        out_specs=[VMEM, VMEM],
        out_shape=[
            jax.ShapeDtypeStruct((width, cols), jnp.float32),
            jax.ShapeDtypeStruct((NY * NX, K * SUB, LANE), jnp.float32),
        ],
        scratch_shapes=[pltpu.VMEM((parts, shards // parts, rows, width), jnp.float32)] * 2
        + [pltpu.VMEM((width, cols), jnp.bfloat16)] * 2
        + [pltpu.SemaphoreType.DMA((2 * parts,))],
        compiler_params=pltpu.CompilerParams(vmem_limit_bytes=28 << 20),
        name="solve",
    )(both, rhs)


def collect_kernel(index_ref, start_ref, parts_ref, out_ref, acc):
    acc[...] = start_ref[...]

    def one(s, carry):
        at = [pl.multiple_of(index_ref[s, k] * SUB, SUB) for k in range(K)]
        new = [acc[pl.ds(at[k], SUB), :] - parts_ref[s, SUB * k : SUB * (k + 1), :] for k in range(K)]
        for k in range(K):
            acc[pl.ds(at[k], SUB), :] = new[k]
        return carry

    lax.fori_loop(0, parts_ref.shape[0], one, 0)
    for x in range(NX):
        out_ref[x] = acc[...]


def collect(index, start, parts):
    return pl.pallas_call(
        collect_kernel,
        in_specs=[SMEM, VMEM, VMEM],
        out_specs=VMEM,
        out_shape=jax.ShapeDtypeStruct((NX, NB * SUB, LANE), jnp.float32),
        scratch_shapes=[pltpu.VMEM((NB * SUB, LANE), jnp.float32)],
        compiler_params=pltpu.CompilerParams(vmem_limit_bytes=12 << 20),
        name="collect",
    )(index, start, parts)


def root_kernel(inv_ref, column_ref, out_ref):
    tiles = [column_ref[x, SUB * b : SUB * (b + 1), :] for b in range(NB) for x in range(NX)]
    hi, lo = split(jnp.concatenate(tiles))
    out = dot3(inv_ref[...].reshape(-1, inv_ref.shape[2]), hi, lo)
    out_ref[...] = out.reshape(out_ref.shape)


def root(inv, column):
    return pl.pallas_call(
        root_kernel,
        in_specs=[VMEM, VMEM],
        out_specs=VMEM,
        out_shape=jax.ShapeDtypeStruct((inv.shape[0], inv.shape[1], LANE), jnp.float32),
        compiler_params=pltpu.CompilerParams(vmem_limit_bytes=12 << 20),
        name="root",
    )(inv, column)


def body(low_rhs, low_inverse, panels, row_blocks, root_rhs, root_inverse):
    own = root_rhs.shape[0]
    y = lax.axis_index("y")

    some = BLK // 4
    by_y = root_inverse.reshape(own, NB, 4, some).transpose(2, 0, 1, 3).reshape(4, 1, own, NB * some)
    inv = lax.all_to_all(jnp.broadcast_to(by_y, (4, 2, own, NB * some)).reshape(NY, own, NB * some), "y", 0, 0)
    rhs_tiles = root_rhs.reshape(2, NX, SUB, 2, LANE).transpose(0, 3, 1, 2, 4)
    rhs_tiles = jnp.broadcast_to(rhs_tiles[None], (2, 2, 2, NX, SUB, LANE))
    blocks = jnp.pad(row_blocks.astype(jnp.float32), ((0, SUB - 1), (0, LANE - K)))
    early = jnp.concatenate(
        [rhs_tiles.reshape(NY * NX, SUB, LANE), jnp.broadcast_to(blocks[None], (NY * NX, SUB, LANE))], axis=1
    )
    early = lax.all_to_all(early, LEAF, 0, 0)
    index = early[:, SUB, :K].astype(jnp.int32)
    start = lax.dynamic_index_in_dim(early[:, :SUB].reshape(NB, 2, SUB, LANE), y // 4, 1, keepdims=False)
    start = start.reshape(NB * SUB, LANE)

    both = lax.all_gather(jnp.concatenate([low_inverse, panels]), GRP, axis=0)
    both, inv, index, start = lax.optimization_barrier((both, inv, index, start))

    low_solution, tiles = solve(both, low_rhs)
    parts = lax.all_to_all(tiles, LEAF, 0, 0)
    column = lax.all_to_all(collect(index, start, parts), "x", 0, 0)
    pieces = lax.all_to_all(root(inv, column), "y", 0, 0)
    halves = jnp.sum(pieces.reshape(4, 2, own, LANE), axis=0)
    return (low_solution, jnp.concatenate([halves[0], halves[1]], axis=1))


def solution(mesh):
    fine = Mesh(mesh.devices.reshape(NY, NX, NZ, NC), LEAF + GRP)
    placed = (
        P(LEAF, GRP),
        P(LEAF + GRP, None),
        P(LEAF + GRP, None),
        P(LEAF, None),
        P(LEAF, GRP),
        P(LEAF, None),
    )
    return jax.shard_map(
        body,
        mesh=fine,
        in_specs=placed,
        out_specs=(P(LEAF, GRP), P(LEAF, GRP)),
        check_vma=False,
    )
```

```python
import jax
import jax.numpy as jnp
from jax import lax
from jax.experimental import pallas as pl
from jax.experimental.pallas import tpu as pltpu
from jax.sharding import Mesh
from jax.sharding import PartitionSpec as P

BLK = 128
NB = 16
K = 8
NA, NX, NZ, NC = 4, 4, 8, 2
NEAR = 2 * NX
LEAF = ("ya", "yb", "x")
GRP = ("z", "c")
SUB, LANE = 8, 128
VMEM = pl.BlockSpec(memory_space=pltpu.VMEM)
SMEM = pl.BlockSpec(memory_space=pltpu.SMEM)


def split(a):
    hi = a.astype(jnp.bfloat16)
    return hi, (a - hi.astype(jnp.float32)).astype(jnp.bfloat16)


def dot3(a, b_hi, b_lo):
    hi, lo = split(a)
    d = lambda u, v: jnp.dot(u, v, preferred_element_type=jnp.float32)
    return d(hi, b_hi) + (d(hi, b_lo) + d(lo, b_hi))


def solve_kernel(both_ref, rhs_ref, low_ref, tiles_ref, l_buf, p_buf, s_hi, s_lo, sems):
    parts, shards, rows, width = l_buf.shape
    part = shards * rows

    def read(i):
        here = pl.ds(shards * (i % parts), shards)
        if i < parts:
            deep = pl.ds(0, (i + 1) * part)
            src, dst = both_ref.at[here, pl.ds(0, rows), deep], l_buf.at[i, :, :, deep]
        else:
            src, dst = both_ref.at[here, pl.ds(rows, rows), :], p_buf.at[i - parts]
        return pltpu.make_async_copy(src, dst, sems.at[i])

    reads = [read(i) for i in range(2 * parts)]
    for copy in reads:
        copy.start()
    r_hi, r_lo = split(rhs_ref[...])
    for i in range(parts):
        reads[i].wait()
        deep = (i + 1) * part
        s = dot3(l_buf[i].reshape(part, width)[:, :deep], r_hi[:deep], r_lo[:deep])
        here = pl.ds(i * part, part)
        low_ref[here, :] = s
        s_hi[here, :], s_lo[here, :] = split(s)
    for i in range(parts):
        reads[parts + i].wait()
        u = dot3(p_buf[i].reshape(part, width), s_hi[...], s_lo[...])
        for j in range(part // BLK):
            k = i * (part // BLK) + j
            for a in range(NA):
                for near in range(NEAR):
                    r = BLK * j + SUB * (NX * a + near % NX)
                    c = LANE * (near // NX)
                    at = SUB * (NA * k + a)
                    tiles_ref[near, at : at + SUB, :] = u[r : r + SUB, c : c + LANE]


def solve(both, rhs, parts=2):
    shards, rows2, width = both.shape
    rows, cols = rows2 // 2, rhs.shape[1]
    return pl.pallas_call(
        solve_kernel,
        in_specs=[pl.BlockSpec(memory_space=pltpu.HBM), VMEM],
        out_specs=[VMEM, VMEM],
        out_shape=[
            jax.ShapeDtypeStruct((width, cols), jnp.float32),
            jax.ShapeDtypeStruct((NEAR, K * NA * SUB, LANE), jnp.float32),
        ],
        scratch_shapes=[pltpu.VMEM((parts, shards // parts, rows, width), jnp.float32)] * 2
        + [pltpu.VMEM((width, cols), jnp.bfloat16)] * 2
        + [pltpu.SemaphoreType.DMA((2 * parts,))],
        compiler_params=pltpu.CompilerParams(vmem_limit_bytes=52 << 20),
        name="solve",
    )(both, rhs)


def collect_kernel(index_ref, parts_ref, out_ref):
    out_ref[...] = jnp.zeros_like(out_ref)

    def one(s, carry):
        at = [pl.multiple_of(index_ref[s, k] * SUB, SUB) for k in range(K)]
        for a in range(NA):
            new = [
                out_ref[a, pl.ds(at[k], SUB), :] + parts_ref[s, SUB * (NA * k + a) : SUB * (NA * k + a + 1), :]
                for k in range(K)
            ]
            for k in range(K):
                out_ref[a, pl.ds(at[k], SUB), :] = new[k]
        return carry

    lax.fori_loop(0, parts_ref.shape[0], one, 0)


def collect(index, parts):
    return pl.pallas_call(
        collect_kernel,
        in_specs=[SMEM, VMEM],
        out_specs=VMEM,
        out_shape=jax.ShapeDtypeStruct((NA, NB * SUB, LANE), jnp.float32),
        compiler_params=pltpu.CompilerParams(vmem_limit_bytes=12 << 20),
        name="collect",
    )(index, parts)


def root_kernel(inv_ref, column_ref, out_ref):
    tiles = [column_ref[x, SUB * b : SUB * (b + 1), :] for b in range(NB) for x in range(NX)]
    hi, lo = split(jnp.concatenate(tiles))
    out = dot3(inv_ref[...].reshape(-1, inv_ref.shape[2]), hi, lo)
    out_ref[...] = out.reshape(out_ref.shape)


def root(inv, column):
    return pl.pallas_call(
        root_kernel,
        in_specs=[VMEM, VMEM],
        out_specs=VMEM,
        out_shape=jax.ShapeDtypeStruct((inv.shape[0], inv.shape[1], LANE), jnp.float32),
        compiler_params=pltpu.CompilerParams(vmem_limit_bytes=12 << 20),
        name="root",
    )(inv, column)


def body(low_rhs, low_inverse, panels, row_blocks, root_rhs, root_inverse):
    own = root_rhs.shape[0]
    ya = lax.axis_index("ya")

    some = BLK // NA
    by_ya = root_inverse.reshape(own, NB, NA, some).transpose(2, 0, 1, 3).reshape(NA, 1, own, NB * some)
    by_y = jnp.broadcast_to(by_ya, (NA, 2, own, NB * some)).reshape(2 * NA, own, NB * some)
    inv = lax.all_to_all(by_y, ("ya", "yb"), 0, 0)
    rhs_tiles = root_rhs.reshape(2, NX, SUB, 2, LANE).transpose(0, 3, 1, 2, 4)
    rhs_tiles = jnp.broadcast_to(rhs_tiles[None], (2, 2, 2, NX, SUB, LANE))
    blocks = jnp.pad(row_blocks.astype(jnp.float32), ((0, SUB - 1), (0, LANE - K)))
    early = jnp.concatenate(
        [rhs_tiles.reshape(NA * NEAR, SUB, LANE), jnp.broadcast_to(blocks[None], (NA * NEAR, SUB, LANE))], axis=1
    )
    early = lax.all_to_all(early, LEAF, 0, 0)
    index = lax.dynamic_slice_in_dim(early[:, SUB, :K].astype(jnp.int32), NEAR * ya, NEAR)
    start = lax.dynamic_index_in_dim(early[:, :SUB].reshape(NB, 2, SUB, LANE), ya // 2, 1, keepdims=False)
    start = start.reshape(NB * SUB, LANE)

    both = lax.all_gather(jnp.concatenate([low_inverse, panels]), GRP, axis=0)
    both, inv, index, start = lax.optimization_barrier((both, inv, index, start))

    low_solution, tiles = solve(both, low_rhs)
    parts = lax.all_to_all(tiles, ("yb", "x"), 0, 0)
    sums = lax.all_to_all(collect(index, parts), "ya", 0, 0)
    combined = start - jnp.sum(sums, axis=0)
    column = lax.all_to_all(jnp.broadcast_to(combined[None], (NX, NB * SUB, LANE)), "x", 0, 0)
    pieces = lax.all_to_all(root(inv, column), ("ya", "yb"), 0, 0)
    halves = jnp.sum(pieces.reshape(NA, 2, own, LANE), axis=0)
    return (low_solution, jnp.concatenate([halves[0], halves[1]], axis=1))


def solution(mesh):
    fine = Mesh(mesh.devices.reshape(NA, 2, NX, NZ, NC), LEAF + GRP)
    placed = (
        P(LEAF, GRP),
        P(LEAF + GRP, None),
        P(LEAF + GRP, None),
        P(LEAF, None),
        P(LEAF, GRP),
        P(LEAF, None),
    )
    return jax.shard_map(
        body,
        mesh=fine,
        in_specs=placed,
        out_specs=(P(LEAF, GRP), P(LEAF, GRP)),
        check_vma=False,
    )
```

```python
import jax
import jax.numpy as jnp
from jax import lax
from jax.experimental import pallas as pl
from jax.experimental.pallas import tpu as pltpu
from jax.sharding import Mesh
from jax.sharding import PartitionSpec as P

BLK = 128
NB = 16
K = 8
NA, NX, NZ, NC = 4, 4, 8, 2
NEAR = 2 * NX
LEAF = ("ya", "yb", "x")
GRP = ("z", "c")
SUB, LANE = 8, 128
VMEM = pl.BlockSpec(memory_space=pltpu.VMEM)
SMEM = pl.BlockSpec(memory_space=pltpu.SMEM)


def split(a):
    hi = a.astype(jnp.bfloat16)
    return hi, (a - hi.astype(jnp.float32)).astype(jnp.bfloat16)


def dot3(a, b_hi, b_lo):
    hi, lo = split(a)
    d = lambda u, v: jnp.dot(u, v, preferred_element_type=jnp.float32)
    return d(hi, b_hi) + (d(hi, b_lo) + d(lo, b_hi))


def solve_kernel(both_ref, r_hi, r_lo, low_ref, tiles_ref, pieces, hi, lo, s_hi, s_lo, low, sems, low_sem):
    count, shards, rows, width = pieces.shape
    parts = count // 2
    part = shards * rows
    deep = [min((i + 1) * part, width) for i in range(count)]

    def read(i):
        here, which = pl.ds(shards * (i % parts), shards), pl.ds(rows * (i // parts), rows)
        depth = pl.ds(0, deep[i])
        return pltpu.make_async_copy(both_ref.at[here, which, depth], pieces.at[i, :, :, depth], sems.at[i])

    reads = [read(i) for i in range(count)]
    for copy in reads:
        copy.start()
    d = lambda u, v: jnp.dot(u, v, preferred_element_type=jnp.float32)

    def cut(i):
        hi[i, :, : deep[i]], lo[i, :, : deep[i]] = split(pieces[i].reshape(part, width)[:, : deep[i]])

    reads[0].wait()
    cut(0)
    for i in range(count):
        if i + 1 < count:
            reads[i + 1].wait()
            cut(i + 1)
        n = deep[i]
        a_hi, a_lo = hi[i, :, :n], lo[i, :, :n]
        b_hi, b_lo = (r_hi[:n], r_lo[:n]) if i < parts else (s_hi[...], s_lo[...])
        out = d(a_hi, b_hi) + (d(a_hi, b_lo) + d(a_lo, b_hi))
        if i < parts:
            here = pl.ds(i * part, part)
            low[here, :] = out
            s_hi[here, :], s_lo[here, :] = split(out)
        if i == parts - 1:
            done = pltpu.make_async_copy(low, low_ref, low_sem)
            done.start()
        if i >= parts:
            for j in range(part // BLK):
                k = (i - parts) * (part // BLK) + j
                for a in range(NA):
                    for near in range(NEAR):
                        r = BLK * j + SUB * (NX * a + near % NX)
                        c = LANE * (near // NX)
                        at = SUB * (NA * k + a)
                        tiles_ref[near, at : at + SUB, :] = out[r : r + SUB, c : c + LANE]
    done.wait()


def solve(both, rhs_hi, rhs_lo, parts=2):
    shards, rows2, width = both.shape
    rows, cols = rows2 // 2, rhs_hi.shape[1]
    part = width // parts
    return pl.pallas_call(
        solve_kernel,
        in_specs=[pl.BlockSpec(memory_space=pltpu.HBM), VMEM, VMEM],
        out_specs=[pl.BlockSpec(memory_space=pltpu.HBM), VMEM],
        out_shape=[
            jax.ShapeDtypeStruct((width, cols), jnp.float32),
            jax.ShapeDtypeStruct((NEAR, K * NA * SUB, LANE), jnp.float32),
        ],
        scratch_shapes=[pltpu.VMEM((2 * parts, shards // parts, rows, width), jnp.float32)]
        + [pltpu.VMEM((2 * parts, part, width), jnp.bfloat16)] * 2
        + [pltpu.VMEM((width, cols), jnp.bfloat16)] * 2
        + [pltpu.VMEM((width, cols), jnp.float32)]
        + [pltpu.SemaphoreType.DMA((2 * parts,)), pltpu.SemaphoreType.DMA(())],
        compiler_params=pltpu.CompilerParams(vmem_limit_bytes=52 << 20),
        name="solve",
    )(both, rhs_hi, rhs_lo)


def split_kernel(a_ref, hi_ref, lo_ref):
    hi_ref[...], lo_ref[...] = split(a_ref[...])


def split_ahead(a):
    return pl.pallas_call(
        split_kernel,
        in_specs=[VMEM],
        out_specs=[VMEM, VMEM],
        out_shape=[jax.ShapeDtypeStruct(a.shape, jnp.bfloat16)] * 2,
        compiler_params=pltpu.CompilerParams(vmem_limit_bytes=12 << 20),
        name="split_ahead",
    )(a)


def collect_kernel(index_ref, parts_ref, out_ref):
    out_ref[...] = jnp.zeros_like(out_ref)

    def one(s, carry):
        at = [pl.multiple_of(index_ref[s, k] * SUB, SUB) for k in range(K)]
        for a in range(NA):
            new = [
                out_ref[a, pl.ds(at[k], SUB), :] + parts_ref[s, SUB * (NA * k + a) : SUB * (NA * k + a + 1), :]
                for k in range(K)
            ]
            for k in range(K):
                out_ref[a, pl.ds(at[k], SUB), :] = new[k]
        return carry

    lax.fori_loop(0, parts_ref.shape[0], one, 0)


def collect(index, parts):
    return pl.pallas_call(
        collect_kernel,
        in_specs=[SMEM, VMEM],
        out_specs=VMEM,
        out_shape=jax.ShapeDtypeStruct((NA, NB * SUB, LANE), jnp.float32),
        compiler_params=pltpu.CompilerParams(vmem_limit_bytes=12 << 20),
        name="collect",
    )(index, parts)


def root_kernel(inv_ref, column_ref, out_ref):
    tiles = [column_ref[x, SUB * b : SUB * (b + 1), :] for b in range(NB) for x in range(NX)]
    hi, lo = split(jnp.concatenate(tiles))
    out = dot3(inv_ref[...].reshape(-1, inv_ref.shape[2]), hi, lo)
    out_ref[...] = out.reshape(out_ref.shape)


def root(inv, column):
    return pl.pallas_call(
        root_kernel,
        in_specs=[VMEM, VMEM],
        out_specs=VMEM,
        out_shape=jax.ShapeDtypeStruct((inv.shape[0], inv.shape[1], LANE), jnp.float32),
        compiler_params=pltpu.CompilerParams(vmem_limit_bytes=12 << 20),
        name="root",
    )(inv, column)


def body(low_rhs, low_inverse, panels, row_blocks, root_rhs, root_inverse):
    own = root_rhs.shape[0]
    ya = lax.axis_index("ya")

    some = BLK // NA
    by_ya = root_inverse.reshape(own, NB, NA, some).transpose(2, 0, 1, 3).reshape(NA, 1, own, NB * some)
    by_y = jnp.broadcast_to(by_ya, (NA, 2, own, NB * some)).reshape(2 * NA, own, NB * some)
    inv = lax.all_to_all(by_y, ("ya", "yb"), 0, 0)
    rhs_tiles = root_rhs.reshape(2, NX, SUB, 2, LANE).transpose(0, 3, 1, 2, 4)
    rhs_tiles = jnp.broadcast_to(rhs_tiles[None], (2, 2, 2, NX, SUB, LANE))
    blocks = jnp.pad(row_blocks.astype(jnp.float32), ((0, SUB - 1), (0, LANE - K)))
    early = jnp.concatenate(
        [rhs_tiles.reshape(NA * NEAR, SUB, LANE), jnp.broadcast_to(blocks[None], (NA * NEAR, SUB, LANE))], axis=1
    )
    early = lax.all_to_all(early, LEAF, 0, 0)
    index = lax.dynamic_slice_in_dim(early[:, SUB, :K].astype(jnp.int32), NEAR * ya, NEAR)
    start = lax.dynamic_index_in_dim(early[:, :SUB].reshape(NB, 2, SUB, LANE), ya // 2, 1, keepdims=False)
    start = start.reshape(NB * SUB, LANE)

    both = lax.all_gather(jnp.concatenate([low_inverse, panels]), GRP, axis=0)
    rhs_hi, rhs_lo = split_ahead(low_rhs)
    both, inv, index, start, rhs_hi, rhs_lo = lax.optimization_barrier((both, inv, index, start, rhs_hi, rhs_lo))

    low_solution, tiles = solve(both, rhs_hi, rhs_lo)
    parts = lax.all_to_all(tiles, ("yb", "x"), 0, 0)
    sums = lax.all_to_all(collect(index, parts), "ya", 0, 0)
    combined = start - jnp.sum(sums, axis=0)
    column = lax.all_to_all(jnp.broadcast_to(combined[None], (NX, NB * SUB, LANE)), "x", 0, 0)
    pieces = lax.all_to_all(root(inv, column), ("ya", "yb"), 0, 0)
    halves = jnp.sum(pieces.reshape(NA, 2, own, LANE), axis=0)
    return (low_solution, jnp.concatenate([halves[0], halves[1]], axis=1))


def solution(mesh):
    fine = Mesh(mesh.devices.reshape(NA, 2, NX, NZ, NC), LEAF + GRP)
    placed = (
        P(LEAF, GRP),
        P(LEAF + GRP, None),
        P(LEAF + GRP, None),
        P(LEAF, None),
        P(LEAF, GRP),
        P(LEAF, None),
    )
    return jax.shard_map(
        body,
        mesh=fine,
        in_specs=placed,
        out_specs=(P(LEAF, GRP), P(LEAF, GRP)),
        check_vma=False,
    )
```

```python
import jax
import jax.numpy as jnp
from jax import lax
from jax.experimental import pallas as pl
from jax.experimental.pallas import tpu as pltpu
from jax.sharding import Mesh
from jax.sharding import PartitionSpec as P

BLK = 128
NB = 16
K = 8
NA, NX, NZ, NC = 4, 4, 8, 2
NEAR = 2 * NX
LEAF = ("ya", "yb", "x")
GRP = ("z", "c")
SUB, LANE = 8, 128
VMEM = pl.BlockSpec(memory_space=pltpu.VMEM)
SMEM = pl.BlockSpec(memory_space=pltpu.SMEM)


def split(a):
    hi = a.astype(jnp.bfloat16)
    return hi, (a - hi.astype(jnp.float32)).astype(jnp.bfloat16)


def dot3(a, b_hi, b_lo):
    hi, lo = split(a)
    d = lambda u, v: jnp.dot(u, v, preferred_element_type=jnp.float32)
    return d(hi, b_hi) + (d(hi, b_lo) + d(lo, b_hi))


def solve_kernel(both_ref, r_hi, r_lo, low_ref, tiles_ref, pieces, hi, lo, s_hi, s_lo, low, sems, low_sem):
    count, shards, rows, width = pieces.shape
    parts = count // 2
    part = shards * rows
    deep = [min((i + 1) * part, width) for i in range(count)]

    def read(i):
        here = pl.ds(shards * (i % parts), shards)
        src = both_ref.at[here, :, pl.ds(width * (i // parts), deep[i])]
        return pltpu.make_async_copy(src, pieces.at[i, :, :, pl.ds(0, deep[i])], sems.at[i])

    reads = [read(i) for i in range(count)]
    for copy in reads:
        copy.start()
    d = lambda u, v: jnp.dot(u, v, preferred_element_type=jnp.float32)

    def cut(i):
        hi[i, :, : deep[i]], lo[i, :, : deep[i]] = split(pieces[i].reshape(part, width)[:, : deep[i]])

    reads[0].wait()
    cut(0)
    for i in range(count):
        if i + 1 < count:
            reads[i + 1].wait()
            cut(i + 1)
        n = deep[i]
        a_hi, a_lo = hi[i, :, :n], lo[i, :, :n]
        b_hi, b_lo = (r_hi[:n], r_lo[:n]) if i < parts else (s_hi[...], s_lo[...])
        out = d(a_hi, b_hi) + (d(a_hi, b_lo) + d(a_lo, b_hi))
        if i < parts:
            here = pl.ds(i * part, part)
            low[here, :] = out
            s_hi[here, :], s_lo[here, :] = split(out)
        if i == parts - 1:
            done = pltpu.make_async_copy(low, low_ref, low_sem)
            done.start()
        if i >= parts:
            for j in range(part // BLK):
                k = (i - parts) * (part // BLK) + j
                for a in range(NA):
                    for near in range(NEAR):
                        r = BLK * j + SUB * (NX * a + near % NX)
                        c = LANE * (near // NX)
                        at = SUB * (NA * k + a)
                        tiles_ref[near, at : at + SUB, :] = out[r : r + SUB, c : c + LANE]
    done.wait()


def solve(both, rhs_hi, rhs_lo, parts=2):
    shards, rows, _ = both.shape
    width, cols = rhs_hi.shape
    part = width // parts
    return pl.pallas_call(
        solve_kernel,
        in_specs=[pl.BlockSpec(memory_space=pltpu.HBM), VMEM, VMEM],
        out_specs=[pl.BlockSpec(memory_space=pltpu.HBM), VMEM],
        out_shape=[
            jax.ShapeDtypeStruct((width, cols), jnp.float32),
            jax.ShapeDtypeStruct((NEAR, K * NA * SUB, LANE), jnp.float32),
        ],
        scratch_shapes=[pltpu.VMEM((2 * parts, shards // parts, rows, width), jnp.float32)]
        + [pltpu.VMEM((2 * parts, part, width), jnp.bfloat16)] * 2
        + [pltpu.VMEM((width, cols), jnp.bfloat16)] * 2
        + [pltpu.VMEM((width, cols), jnp.float32)]
        + [pltpu.SemaphoreType.DMA((2 * parts,)), pltpu.SemaphoreType.DMA(())],
        compiler_params=pltpu.CompilerParams(vmem_limit_bytes=52 << 20),
        name="solve",
    )(both, rhs_hi, rhs_lo)


def split_kernel(a_ref, hi_ref, lo_ref):
    hi_ref[...], lo_ref[...] = split(a_ref[...])


def split_ahead(a):
    return pl.pallas_call(
        split_kernel,
        in_specs=[VMEM],
        out_specs=[VMEM, VMEM],
        out_shape=[jax.ShapeDtypeStruct(a.shape, jnp.bfloat16)] * 2,
        compiler_params=pltpu.CompilerParams(vmem_limit_bytes=12 << 20),
        name="split_ahead",
    )(a)


def collect_kernel(index_ref, parts_ref, out_ref):
    out_ref[...] = jnp.zeros_like(out_ref)

    def one(s, carry):
        at = [pl.multiple_of(index_ref[s, k] * SUB, SUB) for k in range(K)]
        for a in range(NA):
            new = [
                out_ref[a, pl.ds(at[k], SUB), :] + parts_ref[s, SUB * (NA * k + a) : SUB * (NA * k + a + 1), :]
                for k in range(K)
            ]
            for k in range(K):
                out_ref[a, pl.ds(at[k], SUB), :] = new[k]
        return carry

    lax.fori_loop(0, parts_ref.shape[0], one, 0)


def collect(index, parts):
    return pl.pallas_call(
        collect_kernel,
        in_specs=[SMEM, VMEM],
        out_specs=VMEM,
        out_shape=jax.ShapeDtypeStruct((NA, NB * SUB, LANE), jnp.float32),
        compiler_params=pltpu.CompilerParams(vmem_limit_bytes=12 << 20),
        name="collect",
    )(index, parts)


def root_kernel(inv_ref, column_ref, out_ref):
    tiles = [column_ref[x, SUB * b : SUB * (b + 1), :] for b in range(NB) for x in range(NX)]
    hi, lo = split(jnp.concatenate(tiles))
    out = dot3(inv_ref[...].reshape(-1, inv_ref.shape[2]), hi, lo)
    out_ref[...] = out.reshape(out_ref.shape)


def root(inv, column):
    return pl.pallas_call(
        root_kernel,
        in_specs=[VMEM, VMEM],
        out_specs=VMEM,
        out_shape=jax.ShapeDtypeStruct((inv.shape[0], inv.shape[1], LANE), jnp.float32),
        compiler_params=pltpu.CompilerParams(vmem_limit_bytes=12 << 20),
        name="root",
    )(inv, column)


def body(low_rhs, low_inverse, panels, row_blocks, root_rhs, root_inverse):
    own = root_rhs.shape[0]
    ya = lax.axis_index("ya")

    some = BLK // NA
    by_ya = root_inverse.reshape(own, NB, NA, some).transpose(2, 0, 1, 3).reshape(NA, 1, own, NB * some)
    by_y = jnp.broadcast_to(by_ya, (NA, 2, own, NB * some)).reshape(2 * NA, own, NB * some)
    inv = lax.all_to_all(by_y, ("ya", "yb"), 0, 0)
    rhs_tiles = root_rhs.reshape(2, NX, SUB, 2, LANE).transpose(0, 3, 1, 2, 4)
    rhs_tiles = jnp.broadcast_to(rhs_tiles[None], (2, 2, 2, NX, SUB, LANE))
    blocks = jnp.pad(row_blocks.astype(jnp.float32), ((0, SUB - 1), (0, LANE - K)))
    early = jnp.concatenate(
        [rhs_tiles.reshape(NA * NEAR, SUB, LANE), jnp.broadcast_to(blocks[None], (NA * NEAR, SUB, LANE))], axis=1
    )
    early = lax.all_to_all(early, LEAF, 0, 0)
    index = lax.dynamic_slice_in_dim(early[:, SUB, :K].astype(jnp.int32), NEAR * ya, NEAR)
    start = lax.dynamic_index_in_dim(early[:, :SUB].reshape(NB, 2, SUB, LANE), ya // 2, 1, keepdims=False)
    start = start.reshape(NB * SUB, LANE)

    both = lax.all_gather(jnp.concatenate([low_inverse, panels], axis=1), GRP, axis=0)
    rhs_hi, rhs_lo = split_ahead(low_rhs)
    both, inv, index, start, rhs_hi, rhs_lo = lax.optimization_barrier((both, inv, index, start, rhs_hi, rhs_lo))

    low_solution, tiles = solve(both, rhs_hi, rhs_lo)
    parts = lax.all_to_all(tiles, ("yb", "x"), 0, 0)
    sums = lax.all_to_all(collect(index, parts), "ya", 0, 0)
    combined = start - jnp.sum(sums, axis=0)
    column = lax.all_to_all(jnp.broadcast_to(combined[None], (NX, NB * SUB, LANE)), "x", 0, 0)
    pieces = lax.all_to_all(root(inv, column), ("ya", "yb"), 0, 0)
    halves = jnp.sum(pieces.reshape(NA, 2, own, LANE), axis=0)
    return (low_solution, jnp.concatenate([halves[0], halves[1]], axis=1))


def solution(mesh):
    fine = Mesh(mesh.devices.reshape(NA, 2, NX, NZ, NC), LEAF + GRP)
    placed = (
        P(LEAF, GRP),
        P(LEAF + GRP, None),
        P(LEAF + GRP, None),
        P(LEAF, None),
        P(LEAF, GRP),
        P(LEAF, None),
    )
    return jax.shard_map(
        body,
        mesh=fine,
        in_specs=placed,
        out_specs=(P(LEAF, GRP), P(LEAF, GRP)),
        check_vma=False,
    )
```

```python
import jax
import jax.numpy as jnp
from jax import lax
from jax.experimental import pallas as pl
from jax.experimental.pallas import tpu as pltpu
from jax.sharding import Mesh
from jax.sharding import PartitionSpec as P

BLK = 128
NB = 16
K = 8
NA, NX, NZ, NC = 4, 4, 8, 2
NEAR = 2 * NX
LEAF = ("ya", "yb", "x")
GRP = ("z", "c")
SUB, LANE = 8, 128
VMEM = pl.BlockSpec(memory_space=pltpu.VMEM)
SMEM = pl.BlockSpec(memory_space=pltpu.SMEM)


def split(a):
    hi = a.astype(jnp.bfloat16)
    return hi, (a - hi.astype(jnp.float32)).astype(jnp.bfloat16)


def dot3(a, b_hi, b_lo):
    hi, lo = split(a)
    d = lambda u, v: jnp.dot(u, v, preferred_element_type=jnp.float32)
    return d(hi, b_hi) + (d(hi, b_lo) + d(lo, b_hi))


def solve_kernel(both_ref, r_hi, r_lo, low_ref, tiles_ref, pieces, hi, lo, s_hi, s_lo, low, sems, low_sem):
    count, shards, rows, width = pieces.shape
    parts = count // 2
    part = shards * rows
    deep = [min((i + 1) * part, width) for i in range(count)]

    def read(i):
        here = pl.ds(shards * (i % parts), shards)
        src = both_ref.at[here, :, pl.ds(width * (i // parts), deep[i])]
        return pltpu.make_async_copy(src, pieces.at[i, :, :, pl.ds(0, deep[i])], sems.at[i])

    reads = [read(i) for i in range(count)]
    for copy in reads:
        copy.start()
    d = lambda u, v: jnp.dot(u, v, preferred_element_type=jnp.float32)

    def cut(i):
        hi[i, :, : deep[i]], lo[i, :, : deep[i]] = split(pieces[i].reshape(part, width)[:, : deep[i]])

    reads[0].wait()
    cut(0)
    for i in range(count):
        if i + 1 < count:
            reads[i + 1].wait()
            cut(i + 1)
        n = deep[i]
        a_hi, a_lo = hi[i, :, :n], lo[i, :, :n]
        b_hi, b_lo = (r_hi[:n], r_lo[:n]) if i < parts else (s_hi[...], s_lo[...])
        out = d(a_hi, b_hi) + (d(a_hi, b_lo) + d(a_lo, b_hi))
        if i < parts:
            here = pl.ds(i * part, part)
            low[here, :] = out
            s_hi[here, :], s_lo[here, :] = split(out)
        if i == parts - 1:
            done = pltpu.make_async_copy(low, low_ref, low_sem)
            done.start()
        if i >= parts:
            for j in range(part // BLK):
                k = (i - parts) * (part // BLK) + j
                for a in range(NA):
                    for near in range(NEAR):
                        r = BLK * j + SUB * (NX * a + near % NX)
                        c = LANE * (near // NX)
                        at = SUB * (NA * k + a)
                        tiles_ref[near, at : at + SUB, :] = out[r : r + SUB, c : c + LANE]
    done.wait()


def solve(both, rhs_hi, rhs_lo, parts=2):
    shards, rows, _ = both.shape
    width, cols = rhs_hi.shape
    part = width // parts
    return pl.pallas_call(
        solve_kernel,
        in_specs=[pl.BlockSpec(memory_space=pltpu.HBM), VMEM, VMEM],
        out_specs=[pl.BlockSpec(memory_space=pltpu.HBM), VMEM],
        out_shape=[
            jax.ShapeDtypeStruct((width, cols), jnp.float32),
            jax.ShapeDtypeStruct((NEAR, K * NA * SUB, LANE), jnp.float32),
        ],
        scratch_shapes=[pltpu.VMEM((2 * parts, shards // parts, rows, width), jnp.float32)]
        + [pltpu.VMEM((2 * parts, part, width), jnp.bfloat16)] * 2
        + [pltpu.VMEM((width, cols), jnp.bfloat16)] * 2
        + [pltpu.VMEM((width, cols), jnp.float32)]
        + [pltpu.SemaphoreType.DMA((2 * parts,)), pltpu.SemaphoreType.DMA(())],
        compiler_params=pltpu.CompilerParams(vmem_limit_bytes=52 << 20),
        name="solve",
    )(both, rhs_hi, rhs_lo)


def split_kernel(a_ref, hi_ref, lo_ref):
    hi_ref[...], lo_ref[...] = split(a_ref[...])


def split_ahead(a):
    return pl.pallas_call(
        split_kernel,
        in_specs=[VMEM],
        out_specs=[VMEM, VMEM],
        out_shape=[jax.ShapeDtypeStruct(a.shape, jnp.bfloat16)] * 2,
        compiler_params=pltpu.CompilerParams(vmem_limit_bytes=12 << 20),
        name="split_ahead",
    )(a)


def collect_kernel(index_ref, parts_ref, out_ref):
    out_ref[...] = jnp.zeros_like(out_ref)

    def one(s, carry):
        at = [pl.multiple_of(index_ref[s, k] * SUB, SUB) for k in range(K)]
        for a in range(NA):
            new = [
                out_ref[a, pl.ds(at[k], SUB), :] + parts_ref[s, SUB * (NA * k + a) : SUB * (NA * k + a + 1), :]
                for k in range(K)
            ]
            for k in range(K):
                out_ref[a, pl.ds(at[k], SUB), :] = new[k]
        return carry

    lax.fori_loop(0, parts_ref.shape[0], one, 0)


def collect(index, parts):
    return pl.pallas_call(
        collect_kernel,
        in_specs=[SMEM, VMEM],
        out_specs=VMEM,
        out_shape=jax.ShapeDtypeStruct((NA, NB * SUB, LANE), jnp.float32),
        compiler_params=pltpu.CompilerParams(vmem_limit_bytes=12 << 20),
        name="collect",
    )(index, parts)


def root_kernel(inv_hi, inv_lo, column_ref, out_ref):
    tiles = [column_ref[x, SUB * b : SUB * (b + 1), :] for b in range(NB) for x in range(NX)]
    hi, lo = split(jnp.concatenate(tiles))
    a_hi, a_lo = [ref[...].reshape(-1, ref.shape[2]) for ref in (inv_hi, inv_lo)]
    d = lambda u, v: jnp.dot(u, v, preferred_element_type=jnp.float32)
    out = d(a_hi, hi) + (d(a_hi, lo) + d(a_lo, hi))
    out_ref[...] = out.reshape(out_ref.shape)


def root(inv_hi, inv_lo, column):
    return pl.pallas_call(
        root_kernel,
        in_specs=[VMEM, VMEM, VMEM],
        out_specs=VMEM,
        out_shape=jax.ShapeDtypeStruct((inv_hi.shape[0], inv_hi.shape[1], LANE), jnp.float32),
        compiler_params=pltpu.CompilerParams(vmem_limit_bytes=12 << 20),
        name="root",
    )(inv_hi, inv_lo, column)


def body(low_rhs, low_inverse, panels, row_blocks, root_rhs, root_inverse):
    own = root_rhs.shape[0]
    ya = lax.axis_index("ya")

    some = BLK // NA
    by_ya = root_inverse.reshape(own, NB, NA, some).transpose(2, 0, 1, 3).reshape(NA, 1, own, NB * some)
    by_y = jnp.broadcast_to(by_ya, (NA, 2, own, NB * some)).reshape(2 * NA, own, NB * some)
    inv = lax.all_to_all(by_y, ("ya", "yb"), 0, 0)
    rhs_tiles = root_rhs.reshape(2, NX, SUB, 2, LANE).transpose(0, 3, 1, 2, 4)
    rhs_tiles = jnp.broadcast_to(rhs_tiles[None], (2, 2, 2, NX, SUB, LANE))
    blocks = jnp.pad(row_blocks.astype(jnp.float32), ((0, SUB - 1), (0, LANE - K)))
    early = jnp.concatenate(
        [rhs_tiles.reshape(NA * NEAR, SUB, LANE), jnp.broadcast_to(blocks[None], (NA * NEAR, SUB, LANE))], axis=1
    )
    early = lax.all_to_all(early, LEAF, 0, 0)
    index = lax.dynamic_slice_in_dim(early[:, SUB, :K].astype(jnp.int32), NEAR * ya, NEAR)
    start = lax.dynamic_index_in_dim(early[:, :SUB].reshape(NB, 2, SUB, LANE), ya // 2, 1, keepdims=False)
    start = start.reshape(NB * SUB, LANE)

    both = lax.all_gather(jnp.concatenate([low_inverse, panels], axis=1), GRP, axis=0)
    rhs_hi, rhs_lo = split_ahead(low_rhs)
    inv = split_ahead(inv)
    both, inv, index, start, rhs_hi, rhs_lo = lax.optimization_barrier((both, inv, index, start, rhs_hi, rhs_lo))

    low_solution, tiles = solve(both, rhs_hi, rhs_lo)
    parts = lax.all_to_all(tiles, ("yb", "x"), 0, 0)
    sums = lax.all_to_all(collect(index, parts), "ya", 0, 0)
    combined = start - jnp.sum(sums, axis=0)
    column = lax.all_to_all(jnp.broadcast_to(combined[None], (NX, NB * SUB, LANE)), "x", 0, 0)
    pieces = lax.all_to_all(root(*inv, column), ("ya", "yb"), 0, 0)
    halves = jnp.sum(pieces.reshape(NA, 2, own, LANE), axis=0)
    return (low_solution, jnp.concatenate([halves[0], halves[1]], axis=1))


def solution(mesh):
    fine = Mesh(mesh.devices.reshape(NA, 2, NX, NZ, NC), LEAF + GRP)
    placed = (
        P(LEAF, GRP),
        P(LEAF + GRP, None),
        P(LEAF + GRP, None),
        P(LEAF, None),
        P(LEAF, GRP),
        P(LEAF, None),
    )
    return jax.shard_map(
        body,
        mesh=fine,
        in_specs=placed,
        out_specs=(P(LEAF, GRP), P(LEAF, GRP)),
        check_vma=False,
    )
```
